32 devices in a mesh: ka: 16 (over z, x, core), col: 2 (over y).
Axes of the slice: x: 2, y: 2, z: 4, core: 2. Of those that a mesh axis runs over, the one named last changes fastest.
Arguments:
- correlations: bfloat16 [16, 8, 2, 512, 512], P('ka', None, None, 'col')
- gauge: bfloat16 [16, 512, 2, 256], P('ka', 'col'), may hold values from -1 to 1
- neighbours: int32 [16, 8], P('ka'), may hold values from 0 to 15, as said below
- shifts: int32 [16, 8, 3], P('ka'), may hold values from -1 to 1, as said below
Outputs:
- u_next: float32 [16, 512, 2, 256], P('ka', 'col')
- gradient: float32 [16, 2, 256, 256], P('ka', None, 'col')
- omega_od: float32 [], replicated
The draws below stay inside these ranges and needn't reach their ends.
Inputs may be any that keep to these rules, and one draw needn't show every extreme that they name: For each k-point k with grid coordinates g(k) = (k // 16, k // 4 % 4, k % 4) on the 1 x 4 x 4 grid, the 8 entries neighbours[k, :] together with shifts[k, :, :] list the displacements d = +-(1,0,0), +-(0,1,0), +-(0,0,1), +-(1,1,1), each once, in some order: g(neighbours[k,b]) = g(k) + d - shifts[k,b] * (1, 4, 4), with each coordinate inside the grid. shifts[k,b] is the componentwise floor of (g(k) + d) / (1, 4, 4) for the displacement d that neighbours[k,b] names.
All inputs are finite; a program needn't handle non-finite values.
Results may differ from the reference program's by a relative error of at most 0.02.
Values may be sent and summed in bfloat16 or wider, within the bound.
A program may use at most 128 MiB of HBM per device.

```python
import jax
import jax.numpy as jnp
from jax import lax

NB = 512
NW = 256
NBV = 8
NS_STEPS = 3
KPOINT_COUNT = 16
NK1 = 1
NBLK = 2


def shell_table():
    return jnp.array([[1, 0, 0], [-1, 0, 0], [0, 1, 0], [0, -1, 0], [0, 0, 1], [0, 0, -1], [1, 1, 1], [-1, -1, -1]], jnp.int32)


def neighbour_table(key):
    sub = jax.random.fold_in(key, 7)
    keys = jax.random.split(sub, KPOINT_COUNT)
    order = jax.vmap(lambda single: jax.random.permutation(single, NBV))(keys)
    displacement = shell_table()[order]
    kpoint_index = jnp.arange(KPOINT_COUNT, dtype=jnp.int32)
    lattice_positions = jnp.stack([kpoint_index // 16, kpoint_index // 4 % 4, kpoint_index % 4], -1)
    grid_sizes = jnp.array([NK1, 4, 4], jnp.int32)
    target = lattice_positions[:, None, :] + displacement
    wraps = jnp.floor_divide(target, grid_sizes)
    inside = target - wraps * grid_sizes
    index = inside[..., 0] * 16 + inside[..., 1] * 4 + inside[..., 2]
    return (index.astype(jnp.int32), wraps.astype(jnp.int32))


def draw_neighbours(key, part):
    return neighbour_table(key)[0]


def draw_shifts(key, part):
    return neighbour_table(key)[1]


def draw_gauge(key, part):
    first, second = jax.random.split(jax.random.fold_in(key, 17))
    shape = (KPOINT_COUNT, NB, NW)
    real = jax.random.normal(first, shape, jnp.float32)
    imag = jax.random.normal(second, shape, jnp.float32)
    factor = 1.0 / (jnp.sqrt(2.0 * NB) * 1.1 * (1.0 + jnp.sqrt(NW / NB)))
    real, imag = (real * factor, imag * factor)
    high = lax.Precision.HIGHEST
    eye = jnp.eye(NW, dtype=jnp.float32)
    for turn in range(16):
        gram_r = jnp.einsum('krm,krn->kmn', real, real, precision=high) + jnp.einsum('krm,krn->kmn', imag, imag, precision=high)
        gram_i = jnp.einsum('krm,krn->kmn', real, imag, precision=high) - jnp.einsum('krm,krn->kmn', imag, real, precision=high)
        mult_r = (3.0 * eye - gram_r) / 2.0
        mult_i = -gram_i / 2.0
        new_r = jnp.einsum('krm,kmn->krn', real, mult_r, precision=high) - jnp.einsum('krm,kmn->krn', imag, mult_i, precision=high)
        new_i = jnp.einsum('krm,kmn->krn', real, mult_i, precision=high) + jnp.einsum('krm,kmn->krn', imag, mult_r, precision=high)
        real, imag = (new_r, new_i)
    return jnp.clip(jnp.stack([real, imag], 2), -1.0, 1.0).astype(jnp.bfloat16)


def draw_correlations(key, part):
    ramp = 1.0 + 2.0 * jnp.arange(KPOINT_COUNT, dtype=jnp.float32) / (KPOINT_COUNT - 1)
    scale = jnp.sqrt(ramp / NB).reshape(KPOINT_COUNT, 1, 1, 1, 1)
    shape = (KPOINT_COUNT, NBV, 2, NB, NB)
    values = jax.random.normal(jax.random.fold_in(key, 13), shape, jnp.float32)
    return (values * scale).astype(jnp.bfloat16)


def setup_inputs(seed: int = 0) -> dict:
    streams_of = jax.random.split(jax.random.key(seed), 5)
    return {
        "correlations": draw_correlations(jax.random.fold_in(streams_of[4], 71), 0),
        "gauge": draw_gauge(jax.random.fold_in(streams_of[4], 71), 0),
        "neighbours": draw_neighbours(jax.random.fold_in(streams_of[4], 71), 0),
        "shifts": draw_shifts(jax.random.fold_in(streams_of[4], 71), 0),
    }


HIGH = lax.Precision.HIGHEST
MIXING = 0.02
STEP_LENGTH = 0.2

def grid_positions(index):
    return jnp.stack([index // 16, index // 4 % 4, index % 4], -1)

def shell_vector_weights(kpoint_index, neighbour_list, shifts):
    grid_sizes = jnp.array([NK1, 4, 4], jnp.float32)
    fractional_position = (grid_positions(neighbour_list) - grid_positions(kpoint_index)[..., None, :]).astype(jnp.float32) / grid_sizes
    fractional_position = fractional_position + shifts.astype(jnp.float32)
    cart_x = -fractional_position[..., 0] + fractional_position[..., 1] + fractional_position[..., 2]
    cart_y = fractional_position[..., 0] - fractional_position[..., 1] + fractional_position[..., 2]
    cart_z = fractional_position[..., 0] + fractional_position[..., 1] - fractional_position[..., 2]
    return 3.0 / (NBV * (cart_x * cart_x + cart_y * cart_y + cart_z * cart_z))

def cprod(form, ar, ai, br, bi, conj_left, conj_right):
    ar, ai, br, bi = [v.astype(jnp.float32) for v in (ar, ai, br, bi)]
    sign_a = -1.0 if conj_left else 1.0
    sign_b = -1.0 if conj_right else 1.0
    e = lambda p, q: jnp.einsum(form, p, q, precision=HIGH)
    real = e(ar, br) - sign_a * sign_b * e(ai, bi)
    imag = sign_b * e(ar, bi) + sign_a * e(ai, br)
    return (real, imag)

def one_point(items):
    mats, own, near, shell_weights = items
    bf = jnp.bfloat16
    qr, qi = cprod('rw,bcr->bwc', own[:, 0], own[:, 1], mats[:, 0], mats[:, 1], True, False)
    qr, qi = (qr.astype(bf), qi.astype(bf))
    blocks = NB // NBLK
    qbr = qr.reshape(NBV, NW, NBLK, blocks)
    qbi = qi.reshape(NBV, NW, NBLK, blocks)
    nbr_r = near[:, :, 0].reshape(NBV, NBLK, blocks, NW)
    nbr_i = near[:, :, 1].reshape(NBV, NBLK, blocks, NW)
    pr, pi = cprod('bwgc,bgcn->bgwn', qbr, qbi, nbr_r, nbr_i, False, False)
    mtr = lax.optimization_barrier(jnp.sum(pr.astype(bf).astype(jnp.float32), 1)).astype(bf)
    mti = lax.optimization_barrier(jnp.sum(pi.astype(bf).astype(jnp.float32), 1)).astype(bf)
    vr, vi = cprod('brm,bnm->brn', near[:, :, 0], near[:, :, 1], mtr, mti, False, True)
    vr = (shell_weights[:, None, None] * vr).astype(bf)
    vi = (shell_weights[:, None, None] * vi).astype(bf)
    yr, yi = cprod('bji,bjn->in', mats[:, 0], mats[:, 1], vr, vi, False, False)
    mr, mi = (mtr.astype(jnp.float32), mti.astype(jnp.float32))
    wr, wi = (shell_weights[:, None, None] * mr, shell_weights[:, None, None] * mi)
    hr, hi = cprod('bmn,bkn->mk', wr, wi, mr, mi, False, True)
    diag_r = jnp.diagonal(mr, 0, 1, 2)[:, None, :]
    diag_i = jnp.diagonal(mi, 0, 1, 2)[:, None, :]
    rr = mr * diag_r + mi * diag_i
    ri = mi * diag_r - mr * diag_i
    wts = shell_weights[:, None, None]
    gr = 2.0 * lax.optimization_barrier(jnp.sum(wts * (rr - jnp.swapaxes(rr, 1, 2)), 0))
    gi = 2.0 * lax.optimization_barrier(jnp.sum(wts * (ri + jnp.swapaxes(ri, 1, 2)), 0))
    square = mr * mr + mi * mi
    offdiag = lax.optimization_barrier(jnp.sum(square, (1, 2))) - lax.optimization_barrier(jnp.sum(jnp.diagonal(square, 0, 1, 2), 1))
    omega = jnp.sum(shell_weights * offdiag) / (KPOINT_COUNT * NW)
    ur, ui = (own[:, 0].astype(jnp.float32), own[:, 1].astype(jnp.float32))
    uhr, uhi = cprod('rm,mn->rn', ur, ui, hr, hi, False, False)
    ugr, ugi = cprod('rm,mn->rn', ur, ui, gr, gi, False, False)
    xr = ur + MIXING * (yr - uhr) + STEP_LENGTH * ugr
    xi = ui + MIXING * (yi - uhi) + STEP_LENGTH * ugi
    sr, si = cprod('rm,rn->mn', xr, xi, xr, xi, True, False)
    scale = jnp.sqrt(NW / (2.0 * jnp.trace(sr)))
    xr, xi = (xr * scale, xi * scale)
    sr, si = (sr * scale * scale, si * scale * scale)
    eye = jnp.eye(NW, dtype=jnp.float32)
    for turn in range(NS_STEPS):
        xr, xi = cprod('rm,mn->rn', xr, xi, (3.0 * eye - sr) / 2.0, -si / 2.0, False, False)
        if turn + 1 < NS_STEPS:
            sr, si = cprod('rm,rn->mn', xr, xi, xr, xi, True, False)
    return (jnp.stack([xr, xi], 1), jnp.stack([gr, gi], 0), omega)

def reference(correlations, gauge, neighbours, shifts):
    kpoint_index = jnp.arange(KPOINT_COUNT, dtype=jnp.int32)
    shell_weights = shell_vector_weights(kpoint_index, neighbours, shifts)
    near = gauge[neighbours]
    u_next, gradient, omega = lax.map(one_point, (correlations, gauge, near, shell_weights))
    return (u_next, gradient, jnp.sum(omega))
```

```python
import functools

import jax
import jax.numpy as jnp
from jax import lax
from jax.experimental import pallas as pl
from jax.experimental.pallas import tpu as pltpu
from jax.sharding import PartitionSpec as P

NS_STEPS = 3
MIXING = 0.02
STEP_LENGTH = 0.2
MESH = pl.DeviceIdType.MESH
SLOTS = [
    (1, 0, 0),
    (-1, 0, 0),
    (0, 0, 1),
    (0, 0, -1),
    (0, 1, 0),
    (0, -1, 0),
    (1, 1, 1),
    (-1, -1, -1),
]
F32 = jnp.float32
BF = jnp.bfloat16


def slot_weight(disp, grid):
    f = [d / n for d, n in zip(disp, grid)]
    x = -f[0] + f[1] + f[2]
    y = f[0] - f[1] + f[2]
    z = f[0] + f[1] - f[2]
    return 3.0 / (len(SLOTS) * (x * x + y * y + z * z))


def mm(a, b):
    return lax.dot_general(a, b, (((1,), (0,)), ((), ())), preferred_element_type=F32)


def mmt(a, b):
    return lax.dot_general(a, b, (((1,), (1,)), ((), ())), preferred_element_type=F32)


def kernel(
    kpts, ncol, nbr_ref, shift_ref, m_hbm, ut_ref,
    x_out, g_out, om_out,
    mbuf, nbuf, ufull, asend, arecv, part, ab, yt, hh, gg, om,
    xsend, xrecv, gsend, grecv, xb, osend, orecv, which, wsm,
    m_sem, ns_sem, nr_sem, us_sem, ur_sem, as_sem, ar_sem, xs_sem, xr_sem, gs_sem, gr_sem,
    os_sem, or_sem,
):
    k = lax.axis_index("ka")
    c = lax.axis_index("col")
    nslot = len(SLOTS)
    nstep = nslot // ncol
    grid = (kpts // 16, 4, 4)
    width = ut_ref.shape[1]
    rows = ut_ref.shape[2]
    others = [lax.rem(c + off, ncol) for off in range(1, ncol)]
    g = (k // 16, k // 4 % 4, k % 4)

    def local_slot(disp):
        return all(d % n == 0 for d, n in zip(disp, grid))

    def moved_to(disp):
        t = [(g[a] - disp[a] + grid[a]) % grid[a] for a in range(3)]
        return t[0] * 16 + t[1] * 4 + t[2]

    bits = []
    step = 1
    while step < kpts:
        bits.append(step)
        step *= 2

    def flip(pos, bit):
        return pos + bit - 2 * bit * (pos // bit % 2)

    hops = [(k, flip(c, bit)) for bit in (1, 2, 4, 8, 16) if bit < ncol]
    hops += [(flip(k, bit), c) for bit in bits]

    for b in range(nslot):
        pltpu.make_async_copy(m_hbm.at[0, b], mbuf.at[b], m_sem.at[b]).start()

    barrier = pltpu.get_barrier_semaphore()
    partners = [(moved_to(d), c) for d in SLOTS if not local_slot(d)]
    partners += [(k, o) for o in others] + hops
    for who in partners:
        pl.semaphore_signal(barrier, inc=1, device_id=who, device_id_type=MESH)
    pl.semaphore_wait(barrier, len(partners))

    def remote(src, dst, s, r, who):
        return pltpu.make_async_remote_copy(
            src_ref=src, dst_ref=dst, send_sem=s, recv_sem=r, device_id=who, device_id_type=MESH
        )

    ucopies = []
    for i, o in enumerate(others):
        ucopies.append(remote(ut_ref, ufull.at[c], us_sem.at[i], ur_sem.at[i], (k, o)))
        ucopies[i].start()
    ncopies = {}
    for s, disp in enumerate(SLOTS):
        if local_slot(disp):
            continue
        ncopies[s] = remote(ut_ref, nbuf.at[s], ns_sem.at[s], nr_sem.at[s], (moved_to(disp), c))
        ncopies[s].start()
    ufull[c] = ut_ref[...]
    for s, disp in enumerate(SLOTS):
        if local_slot(disp):
            nbuf[s] = ut_ref[...]

    codes = []
    for b in range(nslot):
        nb = nbr_ref[0, b]
        gn = (nb // 16, nb // 4 % 4, nb % 4)
        m = [gn[a] - g[a] + shift_ref[0, b, a] * grid[a] for a in range(3)]
        codes.append(m[0] * 9 + m[1] * 3 + m[2])
    for s, disp in enumerate(SLOTS):
        code = disp[0] * 9 + disp[1] * 3 + disp[2]
        found = jnp.int32(0)
        for b in range(nslot):
            found = jnp.where(codes[b] == code, jnp.int32(b), found)
        which[s] = found
        wsm[s] = jnp.float32(slot_weight(disp, grid))

    for b in range(nslot):
        pltpu.make_async_copy(m_hbm.at[0, b], mbuf.at[b], m_sem.at[b]).wait()

    def product(s):
        b = which[s]
        cr, ci = mbuf[b, 0], mbuf[b, 1]
        nr, ni = nbuf[s, 0], nbuf[s, 1]
        return mm(nr, cr) - mm(ni, ci), mm(nr, ci) + mm(ni, cr)

    acopies = []
    for j in range(nstep):
        for s in range(ncol * j, ncol * (j + 1)):
            if s in ncopies:
                ncopies[s].wait_recv()
        for i, o in enumerate(others):
            n = j * (ncol - 1) + i
            ar, ai = product(ncol * j + o)
            asend[n, 0] = ar.astype(BF)
            asend[n, 1] = ai.astype(BF)
            acopy = remote(asend.at[n], arecv.at[n], as_sem.at[n], ar_sem.at[n], (k, o))
            acopy.start()
            acopies.append(acopy)
        ar, ai = product(ncol * j + c)
        part[j, 0] = ar
        part[j, 1] = ai

    for ucopy in ucopies:
        ucopy.wait_recv()
    row = lax.broadcasted_iota(jnp.int32, (width, width), 0)
    col = lax.broadcasted_iota(jnp.int32, (width, width), 1)
    diag = row == col

    for j in range(nstep):
        w = wsm[ncol * j + c]
        fr, fi = part[j, 0], part[j, 1]
        for n in range(j * (ncol - 1), (j + 1) * (ncol - 1)):
            acopies[n].wait_recv()
            fr = fr + arecv[n, 0].astype(F32)
            fi = fi + arecv[n, 1].astype(F32)
        ab[0] = fr.astype(BF)
        ab[1] = fi.astype(BF)
        tr = jnp.zeros((width, width), F32)
        ti = jnp.zeros((width, width), F32)
        for h in range(ncol):
            span = pl.ds(h * rows, rows)
            ar, ai = ab[0, :, span], ab[1, :, span]
            ur, ui = ufull[h, 0], ufull[h, 1]
            tr = tr + mmt(ar, ur) + mmt(ai, ui)
            ti = ti + mmt(ai, ur) - mmt(ar, ui)
        trb, tib = tr.astype(BF), ti.astype(BF)
        tr, ti = trb.astype(F32), tib.astype(F32)
        mr, mi = tr.T, ti.T
        mrb, mib = mr.astype(BF), mi.astype(BF)
        hr = w * (mm(mrb, trb) + mm(mib, tib))
        hi = w * (mm(mib, trb) - mm(mrb, tib))
        drr = jnp.sum(jnp.where(diag, mr, 0.0), 0, keepdims=True)
        dri = jnp.sum(jnp.where(diag, mi, 0.0), 0, keepdims=True)
        dcr = jnp.sum(jnp.where(diag, mr, 0.0), 1, keepdims=True)
        dci = jnp.sum(jnp.where(diag, mi, 0.0), 1, keepdims=True)
        gr = 2.0 * w * ((mr * drr + mi * dri) - (tr * dcr + ti * dci))
        gi = 2.0 * w * ((mi * drr - mr * dri) + (ti * dcr - tr * dci))
        square = jnp.where(diag, 0.0, mr * mr + mi * mi)
        omj = w * jnp.sum(square, 0, keepdims=True)
        yr = w * (mm(mrb, ab[0]) + mm(mib, ab[1]))
        yi = w * (mm(mrb, ab[1]) - mm(mib, ab[0]))
        if j == 0:
            hh[0], hh[1], gg[0], gg[1], om[...], yt[0], yt[1] = hr, hi, gr, gi, omj, yr, yi
        else:
            hh[0] += hr
            hh[1] += hi
            gg[0] += gr
            gg[1] += gi
            om[...] += omj
            yt[0] += yr
            yt[1] += yi

    kr = (-STEP_LENGTH * gg[0] - MIXING * hh[0]).astype(BF)
    ki = (STEP_LENGTH * gg[1] + MIXING * hh[1]).astype(BF)
    for h in range(ncol):
        span = pl.ds(h * rows, rows)
        ur, ui = ufull[h, 0], ufull[h, 1]
        xsend[h, 0] = (MIXING * yt[0, :, span] + mm(kr, ur) - mm(ki, ui)).astype(BF)
        xsend[h, 1] = (MIXING * yt[1, :, span] + mm(kr, ui) + mm(ki, ur)).astype(BF)
    total = jnp.sum(om[...]) / (kpts * width)
    osend[0] = jnp.full(osend.shape[1:], total, F32)
    ocopies = [remote(osend.at[0], orecv.at[0], os_sem.at[0], or_sem.at[0], hops[0])]
    ocopies[0].start()
    xcopies = []
    for i, o in enumerate(others):
        xcopies.append(remote(xsend, xrecv.at[i], xs_sem.at[i], xr_sem.at[i], (k, o)))
        xcopies[i].start()
    share = width // ncol
    mine = pl.ds(pl.multiple_of(c * share, share), share)
    gcopies = []
    for i, o in enumerate(others):
        theirs = pl.ds(pl.multiple_of(o * share, share), share)
        gsend[i, 0] = gg[0, theirs, :].astype(BF)
        gsend[i, 1] = gg[1, theirs, :].astype(BF)
        gcopies.append(remote(gsend.at[i], grecv.at[i], gs_sem.at[i], gr_sem.at[i], (k, o)))
        gcopies[i].start()

    for turn in range(len(hops)):
        ocopies[turn].wait_recv()
        tile = osend[turn] + orecv[turn]
        if turn + 1 < len(hops):
            osend[turn + 1] = tile
            ocopies.append(
                remote(
                    osend.at[turn + 1],
                    orecv.at[turn + 1],
                    os_sem.at[turn + 1],
                    or_sem.at[turn + 1],
                    hops[turn + 1],
                )
            )
            ocopies[turn + 1].start()
        else:
            om_out[...] = tile

    for xcopy in xcopies:
        xcopy.wait_recv()
    for h in range(ncol):
        for p in range(2):
            v = ufull[h, p].astype(F32) + xsend[h, p].astype(F32)
            for i in range(ncol - 1):
                v = v + xrecv[i, h, p].astype(F32)
            yt[p, :, pl.ds(h * rows, rows)] = v
            xb[h, p] = v.astype(BF)

    def gram():
        sr = jnp.zeros((width, width), F32)
        si = jnp.zeros((width, width), F32)
        for h in range(ncol):
            ar, ai = xb[h, 0], xb[h, 1]
            sr = sr + mmt(ar, ar) + mmt(ai, ai)
            si = si + mmt(ar, ai) - mmt(ai, ar)
        return sr, si

    scale = None
    for turn in range(NS_STEPS):
        sr, si = gram()
        if turn == 0:
            trace = jnp.sum(jnp.where(diag, sr, 0.0), keepdims=True)
            squared = width / (2.0 * trace)
            scale = jnp.sqrt(squared)
            sr, si = sr * squared, si * squared
        er = ((jnp.where(diag, 1.0, 0.0) - sr) / 2.0).astype(BF)
        ei = (-si / 2.0).astype(BF)
        for h in range(ncol):
            span = pl.ds(h * rows, rows)
            ar, ai = xb[h, 0], xb[h, 1]
            vr = yt[0, :, span] + mm(er, ar) + mm(ei, ai)
            vi = yt[1, :, span] + mm(er, ai) - mm(ei, ar)
            if turn == 0:
                vr, vi = vr * scale, vi * scale
            if turn + 1 < NS_STEPS:
                xb[h, 0] = vr.astype(BF)
                xb[h, 1] = vi.astype(BF)
                yt[0, :, span] = vr
                yt[1, :, span] = vi
            else:
                @pl.when(c == h)
                def _():
                    x_out[:, pl.ds(0, width)] = vr.T
                    x_out[:, pl.ds(width, width)] = vi.T

    fr, fi = gg[0, mine, :], gg[1, mine, :]
    for i in range(ncol - 1):
        gcopies[i].wait_recv()
        fr = fr + grecv[i, 0].astype(F32)
        fi = fi + grecv[i, 1].astype(F32)
    g_out[0] = fr
    g_out[1] = fi

    for copy in list(ncopies.values()) + ucopies + acopies + ocopies + xcopies + gcopies:
        copy.wait_send()


def per_device(correlations, gauge, neighbours, shifts):
    kpts = lax.axis_size("ka")
    ncol = lax.axis_size("col")
    _, nslot, _, rows, bands = correlations.shape
    width = gauge.shape[3]
    ut = jnp.transpose(gauge[0], (1, 2, 0))
    rounds = 0
    while 2**rounds < kpts * ncol:
        rounds += 1
    nstep = nslot // ncol
    nsend = nstep * (ncol - 1)
    share = width // ncol
    vm = pltpu.VMEM
    dma = pltpu.SemaphoreType.DMA
    smem = pl.BlockSpec(memory_space=pltpu.SMEM)
    vmem = pl.BlockSpec(memory_space=pltpu.VMEM)
    x, g, om = pl.pallas_call(
        functools.partial(kernel, kpts, ncol),
        out_shape=(
            jax.ShapeDtypeStruct((rows, 2 * width), F32),
            jax.ShapeDtypeStruct((2, share, width), F32),
            jax.ShapeDtypeStruct((8, 128), F32),
        ),
        in_specs=[smem, smem, pl.BlockSpec(memory_space=pl.ANY), vmem],
        out_specs=(vmem, vmem, vmem),
        scratch_shapes=[
            vm((nslot, 2, rows, bands), BF),
            vm((nslot, 2, width, rows), BF),
            vm((ncol, 2, width, rows), BF),
            vm((nsend, 2, width, bands), BF),
            vm((nsend, 2, width, bands), BF),
            vm((nstep, 2, width, bands), F32),
            vm((2, width, bands), BF),
            vm((2, width, bands), F32),
            vm((2, width, width), F32),
            vm((2, width, width), F32),
            vm((1, width), F32),
            vm((ncol, 2, width, rows), BF),
            vm((ncol - 1, ncol, 2, width, rows), BF),
            vm((ncol - 1, 2, share, width), BF),
            vm((ncol - 1, 2, share, width), BF),
            vm((ncol, 2, width, rows), BF),
            vm((rounds, 8, 128), F32),
            vm((rounds, 8, 128), F32),
            pltpu.SMEM((nslot,), jnp.int32),
            pltpu.SMEM((nslot,), F32),
            dma((nslot,)),
            dma((nslot,)),
            dma((nslot,)),
            dma((ncol - 1,)),
            dma((ncol - 1,)),
            dma((nsend,)),
            dma((nsend,)),
            dma((ncol - 1,)),
            dma((ncol - 1,)),
            dma((ncol - 1,)),
            dma((ncol - 1,)),
            dma((rounds,)),
            dma((rounds,)),
        ],
        compiler_params=pltpu.CompilerParams(
            collective_id=0, has_side_effects=True, vmem_limit_bytes=56 * 1024 * 1024
        ),
    )(neighbours, shifts, correlations, ut)
    return (x.reshape(1, rows, 2, width), g[None], om[0, 0])


def solution(mesh):
    return jax.shard_map(
        per_device,
        mesh=mesh,
        in_specs=(
            P("ka", None, None, "col", None),
            P("ka", "col", None, None),
            P("ka", None),
            P("ka", None, None),
        ),
        out_specs=(P("ka", "col", None, None), P("ka", None, "col", None), P()),
        check_vma=False,
    )
```

```python
import functools

import jax
import jax.numpy as jnp
from jax import lax
from jax.experimental import pallas as pl
from jax.experimental.pallas import tpu as pltpu
from jax.sharding import PartitionSpec as P

NS_STEPS = 3
MIXING = 0.02
STEP_LENGTH = 0.2
MESH = pl.DeviceIdType.MESH
CHUNKS = 2
PARTS = 2
SLOTS = [
    (1, 0, 0),
    (-1, 0, 0),
    (0, 0, 1),
    (0, 0, -1),
    (0, 1, 0),
    (0, -1, 0),
    (1, 1, 1),
    (-1, -1, -1),
]
F32 = jnp.float32
BF = jnp.bfloat16


def slot_weight(disp, grid):
    f = [d / n for d, n in zip(disp, grid)]
    x = -f[0] + f[1] + f[2]
    y = f[0] - f[1] + f[2]
    z = f[0] + f[1] - f[2]
    return 3.0 / (len(SLOTS) * (x * x + y * y + z * z))


def mm(a, b):
    return lax.dot_general(a, b, (((1,), (0,)), ((), ())), preferred_element_type=F32)


def mmt(a, b):
    return lax.dot_general(a, b, (((1,), (1,)), ((), ())), preferred_element_type=F32)


def kernel(
    kpts, ncol, nbr_ref, shift_ref, m_hbm, ut_ref,
    x_out, g_out, om_out,
    mbuf, nbuf, ufull, asend, arecv, part, yt, hh, rr, rt, om,
    xsend, xrecv, gsend, grecv, xb, osend, orecv, which, wsm,
    m_sem, ns_sem, nr_sem, us_sem, ur_sem, as_sem, ar_sem, xs_sem, xr_sem, gs_sem, gr_sem,
    os_sem, or_sem,
):
    k = lax.axis_index("ka")
    c = lax.axis_index("col")
    nslot = len(SLOTS)
    nstep = nslot // ncol
    grid = (kpts // 16, 4, 4)
    width = ut_ref.shape[1]
    rows = ut_ref.shape[2]
    others = [lax.rem(c + off, ncol) for off in range(1, ncol)]
    g = (k // 16, k // 4 % 4, k % 4)

    def local_slot(disp):
        return all(d % n == 0 for d, n in zip(disp, grid))

    def moved_to(disp):
        t = [(g[a] - disp[a] + grid[a]) % grid[a] for a in range(3)]
        return t[0] * 16 + t[1] * 4 + t[2]

    bits = []
    step = 1
    while step < kpts:
        bits.append(step)
        step *= 2

    def flip(pos, bit):
        return pos + bit - 2 * bit * (pos // bit % 2)

    hops = [(k, flip(c, bit)) for bit in (1, 2, 4, 8, 16) if bit < ncol]
    hops += [(flip(k, bit), c) for bit in bits]

    for b in range(nslot):
        pltpu.make_async_copy(m_hbm.at[0, b], mbuf.at[b], m_sem.at[b]).start()

    barrier = pltpu.get_barrier_semaphore()
    partners = [(moved_to(d), c) for d in SLOTS if not local_slot(d)]
    partners += [(k, o) for o in others] + hops
    for who in partners:
        pl.semaphore_signal(barrier, inc=1, device_id=who, device_id_type=MESH)
    pl.semaphore_wait(barrier, len(partners))

    def remote(src, dst, s, r, who):
        return pltpu.make_async_remote_copy(
            src_ref=src, dst_ref=dst, send_sem=s, recv_sem=r, device_id=who, device_id_type=MESH
        )

    ucopies = []
    for i, o in enumerate(others):
        ucopies.append(remote(ut_ref, ufull.at[c], us_sem.at[i], ur_sem.at[i], (k, o)))
        ucopies[i].start()
    ncopies = {}
    for s, disp in enumerate(SLOTS):
        if local_slot(disp):
            continue
        ncopies[s] = remote(ut_ref, nbuf.at[s], ns_sem.at[s], nr_sem.at[s], (moved_to(disp), c))
        ncopies[s].start()
    ufull[c] = ut_ref[...]
    for s, disp in enumerate(SLOTS):
        if local_slot(disp):
            nbuf[s] = ut_ref[...]

    codes = []
    for b in range(nslot):
        nb = nbr_ref[0, b]
        gn = (nb // 16, nb // 4 % 4, nb % 4)
        m = [gn[a] - g[a] + shift_ref[a, 0, b] * grid[a] for a in range(3)]
        codes.append(m[0] * 9 + m[1] * 3 + m[2])
    for s, disp in enumerate(SLOTS):
        code = disp[0] * 9 + disp[1] * 3 + disp[2]
        found = jnp.int32(0)
        for b in range(nslot):
            found = jnp.where(codes[b] == code, jnp.int32(b), found)
        which[s] = found
        wsm[s] = jnp.float32(slot_weight(disp, grid))

    for b in range(nslot):
        pltpu.make_async_copy(m_hbm.at[0, b], mbuf.at[b], m_sem.at[b]).wait()

    part_w = width // CHUNKS

    def product(s, q):
        b = which[s]
        cr, ci = mbuf[b, 0], mbuf[b, 1]
        lines = pl.ds(q * part_w, part_w)
        nr, ni = nbuf[s, 0, lines, :], nbuf[s, 1, lines, :]
        return mm(nr, cr) - mm(ni, ci), mm(nr, ci) + mm(ni, cr)

    acopies = {}
    for j in range(nstep):
        for s in range(ncol * j, ncol * (j + 1)):
            if s in ncopies:
                ncopies[s].wait_recv()
        for q in range(CHUNKS):
            for i, o in enumerate(others):
                n = (j * (ncol - 1) + i) * CHUNKS + q
                ar, ai = product(ncol * j + o, q)
                asend[n, 0] = ar.astype(BF)
                asend[n, 1] = ai.astype(BF)
                acopies[n] = remote(
                    asend.at[n], arecv.at[n], as_sem.at[n], ar_sem.at[n], (k, o)
                )
                acopies[n].start()
        for q in range(CHUNKS):
            ar, ai = product(ncol * j + c, q)
            part[j * CHUNKS + q, 0] = ar
            part[j * CHUNKS + q, 1] = ai

    for ucopy in ucopies:
        ucopy.wait_recv()
    row = lax.broadcasted_iota(jnp.int32, (width, width), 0)
    col = lax.broadcasted_iota(jnp.int32, (width, width), 1)
    diag = row == col

    first = True
    for j in range(nstep):
        w = wsm[ncol * j + c]
        for q in range(CHUNKS):
            lines = pl.ds(q * part_w, part_w)
            fr, fi = part[j * CHUNKS + q, 0], part[j * CHUNKS + q, 1]
            for i in range(ncol - 1):
                n = (j * (ncol - 1) + i) * CHUNKS + q
                acopies[n].wait_recv()
                fr = fr + arecv[n, 0].astype(F32)
                fi = fi + arecv[n, 1].astype(F32)
            fr, fi = fr.astype(BF), fi.astype(BF)
            tr = jnp.zeros((part_w, width), F32)
            ti = jnp.zeros((part_w, width), F32)
            for h in range(ncol):
                ar, ai = fr[:, h * rows : (h + 1) * rows], fi[:, h * rows : (h + 1) * rows]
                ur, ui = ufull[h, 0], ufull[h, 1]
                tr = tr + mmt(ar, ur) + mmt(ai, ui)
                ti = ti + mmt(ai, ur) - mmt(ar, ui)
            trb, tib = tr.astype(BF), ti.astype(BF)
            tr, ti = trb.astype(F32), tib.astype(F32)
            mr, mi = tr.T, ti.T
            mrb, mib = mr.astype(BF), mi.astype(BF)
            hr = w * (mm(mrb, trb) + mm(mib, tib))
            hi = w * (mm(mib, trb) - mm(mrb, tib))
            down = row[:, :part_w] == col[:, :part_w] + q * part_w
            over = row[:part_w, :] + q * part_w == col[:part_w, :]
            drr = w * jnp.sum(jnp.where(down, mr, 0.0), 0, keepdims=True)
            dri = w * jnp.sum(jnp.where(down, mi, 0.0), 0, keepdims=True)
            dcr = w * jnp.sum(jnp.where(over, tr, 0.0), 1, keepdims=True)
            dci = w * jnp.sum(jnp.where(over, ti, 0.0), 1, keepdims=True)
            rr0, rr1 = mr * drr + mi * dri, mi * drr - mr * dri
            rt0, rt1 = tr * dcr + ti * dci, ti * dcr - tr * dci
            square = jnp.where(over, 0.0, tr * tr + ti * ti)
            omj = w * jnp.sum(square, 0, keepdims=True)
            yr = w * (mm(mrb, fr) + mm(mib, fi))
            yi = w * (mm(mrb, fi) - mm(mib, fr))
            if j == 0:
                rr[0, :, lines], rr[1, :, lines], rt[0, lines, :], rt[1, lines, :] = (
                    rr0, rr1, rt0, rt1,
                )
            else:
                rr[0, :, lines] += rr0
                rr[1, :, lines] += rr1
                rt[0, lines, :] += rt0
                rt[1, lines, :] += rt1
            if first:
                hh[0], hh[1], om[...], yt[0], yt[1] = hr, hi, omj, yr, yi
            else:
                hh[0] += hr
                hh[1] += hi
                om[...] += omj
                yt[0] += yr
                yt[1] += yi
            first = False

    rr[0] = 2.0 * (rr[0] - rt[0])
    rr[1] = 2.0 * (rr[1] + rt[1])
    kr = (-STEP_LENGTH * rr[0] - MIXING * hh[0]).astype(BF)
    ki = (STEP_LENGTH * rr[1] + MIXING * hh[1]).astype(BF)
    xcopies = {}
    group = ncol // PARTS
    for h in range(ncol):
        span = pl.ds(h * rows, rows)
        ur, ui = ufull[h, 0], ufull[h, 1]
        xsend[h, 0] = (MIXING * yt[0, :, span] + mm(kr, ur) - mm(ki, ui)).astype(BF)
        xsend[h, 1] = (MIXING * yt[1, :, span] + mm(kr, ui) + mm(ki, ur)).astype(BF)
        if h % group == group - 1:
            e = h // group
            piece = pl.ds(e * group, group)
            for i, o in enumerate(others):
                n = i * PARTS + e
                xcopies[n] = remote(
                    xsend.at[piece], xrecv.at[i, piece], xs_sem.at[n], xr_sem.at[n], (k, o)
                )
                xcopies[n].start()
    total = jnp.sum(om[...]) / (kpts * width)
    osend[0] = jnp.full(osend.shape[1:], total, F32)
    ocopies = [remote(osend.at[0], orecv.at[0], os_sem.at[0], or_sem.at[0], hops[0])]
    ocopies[0].start()
    share = width // ncol
    mine = pl.ds(pl.multiple_of(c * share, share), share)
    gcopies = []
    for i, o in enumerate(others):
        theirs = pl.ds(pl.multiple_of(o * share, share), share)
        gsend[i, 0] = rr[0, theirs, :].astype(BF)
        gsend[i, 1] = rr[1, theirs, :].astype(BF)
        gcopies.append(remote(gsend.at[i], grecv.at[i], gs_sem.at[i], gr_sem.at[i], (k, o)))
        gcopies[i].start()

    for turn in range(len(hops)):
        ocopies[turn].wait_recv()
        tile = osend[turn] + orecv[turn]
        if turn + 1 < len(hops):
            osend[turn + 1] = tile
            ocopies.append(
                remote(
                    osend.at[turn + 1],
                    orecv.at[turn + 1],
                    os_sem.at[turn + 1],
                    or_sem.at[turn + 1],
                    hops[turn + 1],
                )
            )
            ocopies[turn + 1].start()
        else:
            om_out[...] = tile

    def gram(hs):
        sr = jnp.zeros((width, width), F32)
        si = jnp.zeros((width, width), F32)
        for h in hs:
            ar, ai = xb[h, 0], xb[h, 1]
            sr = sr + mmt(ar, ar) + mmt(ai, ai)
            si = si + mmt(ar, ai) - mmt(ai, ar)
        return sr, si

    for e in range(PARTS):
        for i in range(ncol - 1):
            xcopies[i * PARTS + e].wait_recv()
        hs = range(e * group, (e + 1) * group)
        for h in hs:
            for p in range(2):
                v = ufull[h, p].astype(F32) + xsend[h, p].astype(F32)
                for i in range(ncol - 1):
                    v = v + xrecv[i, h, p].astype(F32)
                yt[p, :, pl.ds(h * rows, rows)] = v
                xb[h, p] = v.astype(BF)
        sr, si = gram(hs)
        if e == 0:
            hh[0], hh[1] = sr, si
        else:
            hh[0] += sr
            hh[1] += si

    scale = None
    for turn in range(NS_STEPS):
        sr, si = (hh[0], hh[1]) if turn == 0 else gram(range(ncol))
        if turn == 0:
            trace = jnp.sum(jnp.where(diag, sr, 0.0), keepdims=True)
            squared = width / (2.0 * trace)
            scale = jnp.sqrt(squared)
            sr, si = sr * squared, si * squared
        er = ((jnp.where(diag, 1.0, 0.0) - sr) / 2.0).astype(BF)
        ei = (-si / 2.0).astype(BF)
        for h in range(ncol):
            span = pl.ds(h * rows, rows)
            ar, ai = xb[h, 0], xb[h, 1]
            vr = yt[0, :, span] + mm(er, ar) + mm(ei, ai)
            vi = yt[1, :, span] + mm(er, ai) - mm(ei, ar)
            if turn == 0:
                vr, vi = vr * scale, vi * scale
            if turn + 1 < NS_STEPS:
                xb[h, 0] = vr.astype(BF)
                xb[h, 1] = vi.astype(BF)
                yt[0, :, span] = vr
                yt[1, :, span] = vi
            else:
                @pl.when(c == h)
                def _():
                    x_out[0] = vr
                    x_out[1] = vi

    fr, fi = rr[0, mine, :], rr[1, mine, :]
    for i in range(ncol - 1):
        gcopies[i].wait_recv()
        fr = fr + grecv[i, 0].astype(F32)
        fi = fi + grecv[i, 1].astype(F32)
    g_out[0] = fr
    g_out[1] = fi

    for copy in list(ncopies.values()) + ucopies + ocopies + gcopies:
        copy.wait_send()
    for copy in list(acopies.values()) + list(xcopies.values()):
        copy.wait_send()


def place(x_ref, g_ref, om_ref, x_out, g_out, om_out):
    x_out[:, 0, :] = x_ref[0].T
    x_out[:, 1, :] = x_ref[1].T
    g_out[...] = g_ref[...]
    om_out[0, 0] = jnp.max(om_ref[...])


def per_device(correlations, gauge, neighbours, shifts):
    kpts = lax.axis_size("ka")
    ncol = lax.axis_size("col")
    _, nslot, _, rows, bands = correlations.shape
    width = gauge.shape[3]
    ut = jnp.transpose(gauge[0], (1, 2, 0))
    rounds = 0
    while 2**rounds < kpts * ncol:
        rounds += 1
    nstep = nslot // ncol
    nsend = nstep * (ncol - 1) * CHUNKS
    share = width // ncol
    vm = pltpu.VMEM
    dma = pltpu.SemaphoreType.DMA
    smem = pl.BlockSpec(memory_space=pltpu.SMEM)
    vmem = pl.BlockSpec(memory_space=pltpu.VMEM)
    x, g, om = pl.pallas_call(
        functools.partial(kernel, kpts, ncol),
        out_shape=(
            jax.ShapeDtypeStruct((2, width, rows), F32),
            jax.ShapeDtypeStruct((2, share, width), F32),
            jax.ShapeDtypeStruct((8, 128), F32),
        ),
        in_specs=[smem, smem, pl.BlockSpec(memory_space=pl.ANY), vmem],
        out_specs=(vmem, vmem, vmem),
        scratch_shapes=[
            vm((nslot, 2, rows, bands), BF),
            vm((nslot, 2, width, rows), BF),
            vm((ncol, 2, width, rows), BF),
            vm((nsend, 2, width // CHUNKS, bands), BF),
            vm((nsend, 2, width // CHUNKS, bands), BF),
            vm((nstep * CHUNKS, 2, width // CHUNKS, bands), F32),
            vm((2, width, bands), F32),
            vm((2, width, width), F32),
            vm((2, width, width), F32),
            vm((2, width, width), F32),
            vm((1, width), F32),
            vm((ncol, 2, width, rows), BF),
            vm((ncol - 1, ncol, 2, width, rows), BF),
            vm((ncol - 1, 2, share, width), BF),
            vm((ncol - 1, 2, share, width), BF),
            vm((ncol, 2, width, rows), BF),
            vm((rounds, 8, 128), F32),
            vm((rounds, 8, 128), F32),
            pltpu.SMEM((nslot,), jnp.int32),
            pltpu.SMEM((nslot,), F32),
            dma((nslot,)),
            dma((nslot,)),
            dma((nslot,)),
            dma((ncol - 1,)),
            dma((ncol - 1,)),
            dma((nsend,)),
            dma((nsend,)),
            dma(((ncol - 1) * PARTS,)),
            dma(((ncol - 1) * PARTS,)),
            dma((ncol - 1,)),
            dma((ncol - 1,)),
            dma((rounds,)),
            dma((rounds,)),
        ],
        compiler_params=pltpu.CompilerParams(
            collective_id=0, has_side_effects=True, vmem_limit_bytes=56 * 1024 * 1024
        ),
    )(neighbours, jnp.transpose(shifts, (2, 0, 1)), correlations, ut)
    x, g, om = pl.pallas_call(
        place,
        out_shape=(
            jax.ShapeDtypeStruct((rows, 2, width), F32),
            jax.ShapeDtypeStruct((2, share, width), F32),
            jax.ShapeDtypeStruct((1, 1), F32),
        ),
        in_specs=[vmem, vmem, vmem],
        out_specs=(vmem, vmem, smem),
    )(x, g, om)
    return (x[None], g[None], om[0, 0])


def solution(mesh):
    return jax.shard_map(
        per_device,
        mesh=mesh,
        in_specs=(
            P("ka", None, None, "col", None),
            P("ka", "col", None, None),
            P("ka", None),
            P("ka", None, None),
        ),
        out_specs=(P("ka", "col", None, None), P("ka", None, "col", None), P()),
        check_vma=False,
    )
```

```python
import functools

import jax
import jax.numpy as jnp
from jax import lax
from jax.experimental import pallas as pl
from jax.experimental.pallas import tpu as pltpu
from jax.sharding import PartitionSpec as P

NS_STEPS = 3
MIXING = 0.02
STEP_LENGTH = 0.2
MESH = pl.DeviceIdType.MESH
CHUNKS = 1
PARTS = 2
SLOTS = [
    (1, 0, 0),
    (-1, 0, 0),
    (0, 0, 1),
    (0, 0, -1),
    (0, 1, 0),
    (0, -1, 0),
    (1, 1, 1),
    (-1, -1, -1),
]
F32 = jnp.float32
BF = jnp.bfloat16


def slot_weight(disp, grid):
    f = [d / n for d, n in zip(disp, grid)]
    x = -f[0] + f[1] + f[2]
    y = f[0] - f[1] + f[2]
    z = f[0] + f[1] - f[2]
    return 3.0 / (len(SLOTS) * (x * x + y * y + z * z))


def mm(a, b):
    return lax.dot_general(a, b, (((1,), (0,)), ((), ())), preferred_element_type=F32)


def mmt(a, b):
    return lax.dot_general(a, b, (((1,), (1,)), ((), ())), preferred_element_type=F32)


def kernel(
    kpts, ncol, nbr_ref, shift_ref, m_hbm, ut_ref,
    x_out, g_out, om_out,
    mbuf, nbuf, ufull, asend, arecv, part, yt, hh, rr, rt, om,
    xsend, xrecv, gsend, grecv, xb, osend, orecv, which, wsm,
    m_sem, ns_sem, nr_sem, us_sem, ur_sem, as_sem, ar_sem, xs_sem, xr_sem, gs_sem, gr_sem,
    os_sem, or_sem,
):
    k = lax.axis_index("ka")
    c = lax.axis_index("col")
    nslot = len(SLOTS)
    nstep = nslot // ncol
    grid = (kpts // 16, 4, 4)
    width = ut_ref.shape[1]
    rows = ut_ref.shape[2]
    others = [lax.rem(c + off, ncol) for off in range(1, ncol)]
    g = (k // 16, k // 4 % 4, k % 4)

    def local_slot(disp):
        return all(d % n == 0 for d, n in zip(disp, grid))

    def moved_to(disp):
        t = [(g[a] - disp[a] + grid[a]) % grid[a] for a in range(3)]
        return t[0] * 16 + t[1] * 4 + t[2]

    bits = []
    step = 1
    while step < kpts:
        bits.append(step)
        step *= 2

    def flip(pos, bit):
        return pos + bit - 2 * bit * (pos // bit % 2)

    hops = [(k, flip(c, bit)) for bit in (1, 2, 4, 8, 16) if bit < ncol]
    hops += [(flip(k, bit), c) for bit in bits]

    for b in range(nslot):
        pltpu.make_async_copy(m_hbm.at[0, b], mbuf.at[b], m_sem.at[b]).start()

    barrier = pltpu.get_barrier_semaphore()
    partners = [(moved_to(d), c) for d in SLOTS if not local_slot(d)]
    partners += [(k, o) for o in others] + hops
    for who in partners:
        pl.semaphore_signal(barrier, inc=1, device_id=who, device_id_type=MESH)
    pl.semaphore_wait(barrier, len(partners))

    def remote(src, dst, s, r, who):
        return pltpu.make_async_remote_copy(
            src_ref=src, dst_ref=dst, send_sem=s, recv_sem=r, device_id=who, device_id_type=MESH
        )

    ucopies = []
    for i, o in enumerate(others):
        ucopies.append(remote(ut_ref, ufull.at[c], us_sem.at[i], ur_sem.at[i], (k, o)))
        ucopies[i].start()
    singles = [s for s, d in enumerate(SLOTS) if sum(map(abs, d)) == 1 and not local_slot(d)]

    def two_hops(disp):
        for e in singles:
            for f in singles:
                fits = [(SLOTS[e][a] + SLOTS[f][a] - disp[a]) % grid[a] == 0 for a in range(3)]
                if SLOTS[e][1] and SLOTS[f][2] and all(fits):
                    return e, SLOTS[f]
        return None

    ncopies = {}
    relays = {}
    arrived = set()

    def arrive(s):
        if s in ncopies and s not in arrived:
            ncopies[s].wait_recv()
            arrived.add(s)

    for s, disp in enumerate(SLOTS):
        if local_slot(disp):
            continue
        if sum(map(abs, disp)) > 1 and two_hops(disp):
            relays[s] = two_hops(disp)
            continue
        ncopies[s] = remote(ut_ref, nbuf.at[s], ns_sem.at[s], nr_sem.at[s], (moved_to(disp), c))
        ncopies[s].start()
    ufull[c] = ut_ref[...]
    for s, disp in enumerate(SLOTS):
        if local_slot(disp):
            nbuf[s] = ut_ref[...]

    codes = []
    for b in range(nslot):
        nb = nbr_ref[0, b]
        gn = (nb // 16, nb // 4 % 4, nb % 4)
        m = [gn[a] - g[a] + shift_ref[a, 0, b] * grid[a] for a in range(3)]
        codes.append(m[0] * 9 + m[1] * 3 + m[2])
    for s, disp in enumerate(SLOTS):
        code = disp[0] * 9 + disp[1] * 3 + disp[2]
        found = jnp.int32(0)
        for b in range(nslot):
            found = jnp.where(codes[b] == code, jnp.int32(b), found)
        which[s] = found
        wsm[s] = jnp.float32(slot_weight(disp, grid))

    for b in range(nslot):
        pltpu.make_async_copy(m_hbm.at[0, b], mbuf.at[b], m_sem.at[b]).wait()

    part_w = width // CHUNKS

    def product(s, q):
        b = which[s]
        cr, ci = mbuf[b, 0], mbuf[b, 1]
        lines = pl.ds(q * part_w, part_w)
        nr, ni = nbuf[s, 0, lines, :], nbuf[s, 1, lines, :]
        return mm(nr, cr) - mm(ni, ci), mm(nr, ci) + mm(ni, cr)

    acopies = {}

    def relay():
        for s, (e, f) in relays.items():
            arrive(e)
            ncopies[s] = remote(
                nbuf.at[e], nbuf.at[s], ns_sem.at[s], nr_sem.at[s], (moved_to(f), c)
            )
            ncopies[s].start()

    def produce(j):
        for s in range(ncol * j, ncol * (j + 1)):
            arrive(s)
        for q in range(CHUNKS):
            for i, o in enumerate(others):
                n = (j * (ncol - 1) + i) * CHUNKS + q
                ar, ai = product(ncol * j + o, q)
                asend[n, 0] = ar.astype(BF)
                asend[n, 1] = ai.astype(BF)
                acopies[n] = remote(
                    asend.at[n], arecv.at[n], as_sem.at[n], ar_sem.at[n], (k, o)
                )
                acopies[n].start()
        for q in range(CHUNKS):
            ar, ai = product(ncol * j + c, q)
            part[j * CHUNKS + q, 0] = ar
            part[j * CHUNKS + q, 1] = ai

    row = lax.broadcasted_iota(jnp.int32, (width, width), 0)
    col = lax.broadcasted_iota(jnp.int32, (width, width), 1)
    diag = row == col

    def consume(j):
        w = wsm[ncol * j + c]
        for q in range(CHUNKS):
            lines = pl.ds(q * part_w, part_w)
            fr, fi = part[j * CHUNKS + q, 0], part[j * CHUNKS + q, 1]
            for i in range(ncol - 1):
                n = (j * (ncol - 1) + i) * CHUNKS + q
                acopies[n].wait_recv()
                fr = fr + arecv[n, 0].astype(F32)
                fi = fi + arecv[n, 1].astype(F32)
            fr, fi = fr.astype(BF), fi.astype(BF)
            tr = jnp.zeros((part_w, width), F32)
            ti = jnp.zeros((part_w, width), F32)
            for h in range(ncol):
                ar, ai = fr[:, h * rows : (h + 1) * rows], fi[:, h * rows : (h + 1) * rows]
                ur, ui = ufull[h, 0], ufull[h, 1]
                tr = tr + mmt(ar, ur) + mmt(ai, ui)
                ti = ti + mmt(ai, ur) - mmt(ar, ui)
            trb, tib = tr.astype(BF), ti.astype(BF)
            tr, ti = trb.astype(F32), tib.astype(F32)
            mr, mi = tr.T, ti.T
            mrb, mib = mr.astype(BF), mi.astype(BF)
            hr = w * (mm(mrb, trb) + mm(mib, tib))
            hi = w * (mm(mib, trb) - mm(mrb, tib))
            down = row[:, :part_w] == col[:, :part_w] + q * part_w
            over = row[:part_w, :] + q * part_w == col[:part_w, :]
            drr = w * jnp.sum(jnp.where(down, mr, 0.0), 0, keepdims=True)
            dri = w * jnp.sum(jnp.where(down, mi, 0.0), 0, keepdims=True)
            dcr = w * jnp.sum(jnp.where(over, tr, 0.0), 1, keepdims=True)
            dci = w * jnp.sum(jnp.where(over, ti, 0.0), 1, keepdims=True)
            rr0, rr1 = mr * drr + mi * dri, mi * drr - mr * dri
            rt0, rt1 = tr * dcr + ti * dci, ti * dcr - tr * dci
            square = jnp.where(over, 0.0, tr * tr + ti * ti)
            omj = w * jnp.sum(square, 0, keepdims=True)
            yr = w * (mm(mrb, fr) + mm(mib, fi))
            yi = w * (mm(mrb, fi) - mm(mib, fr))
            if j == 0:
                rr[0, :, lines], rr[1, :, lines], rt[0, lines, :], rt[1, lines, :] = (
                    rr0, rr1, rt0, rt1,
                )
            else:
                rr[0, :, lines] += rr0
                rr[1, :, lines] += rr1
                rt[0, lines, :] += rt0
                rt[1, lines, :] += rt1
            if j == 0 and q == 0:
                hh[0], hh[1], om[...], yt[0], yt[1] = hr, hi, omj, yr, yi
            else:
                hh[0] += hr
                hh[1] += hi
                om[...] += omj
                yt[0] += yr
                yt[1] += yi

    for j in range(nstep):
        produce(j)
        if j == 0:
            for ucopy in ucopies:
                ucopy.wait_recv()
        else:
            if j == 1:
                relay()
            consume(j - 1)
    consume(nstep - 1)

    rr[0] = 2.0 * (rr[0] - rt[0])
    rr[1] = 2.0 * (rr[1] + rt[1])
    kr = (-STEP_LENGTH * rr[0] - MIXING * hh[0]).astype(BF)
    ki = (STEP_LENGTH * rr[1] + MIXING * hh[1]).astype(BF)
    xcopies = {}
    group = ncol // PARTS
    for h in range(ncol):
        span = pl.ds(h * rows, rows)
        ur, ui = ufull[h, 0], ufull[h, 1]
        xsend[h, 0] = (MIXING * yt[0, :, span] + mm(kr, ur) - mm(ki, ui)).astype(BF)
        xsend[h, 1] = (MIXING * yt[1, :, span] + mm(kr, ui) + mm(ki, ur)).astype(BF)
        if h % group == group - 1:
            e = h // group
            piece = pl.ds(e * group, group)
            for i, o in enumerate(others):
                n = i * PARTS + e
                xcopies[n] = remote(
                    xsend.at[piece], xrecv.at[i, piece], xs_sem.at[n], xr_sem.at[n], (k, o)
                )
                xcopies[n].start()
    total = jnp.sum(om[...]) / (kpts * width)
    osend[0] = jnp.full(osend.shape[1:], total, F32)
    ocopies = [remote(osend.at[0], orecv.at[0], os_sem.at[0], or_sem.at[0], hops[0])]
    ocopies[0].start()
    share = width // ncol
    mine = pl.ds(pl.multiple_of(c * share, share), share)
    gcopies = []
    for i, o in enumerate(others):
        theirs = pl.ds(pl.multiple_of(o * share, share), share)
        gsend[i, 0] = rr[0, theirs, :].astype(BF)
        gsend[i, 1] = rr[1, theirs, :].astype(BF)
        gcopies.append(remote(gsend.at[i], grecv.at[i], gs_sem.at[i], gr_sem.at[i], (k, o)))
        gcopies[i].start()

    for turn in range(len(hops)):
        ocopies[turn].wait_recv()
        tile = osend[turn] + orecv[turn]
        if turn + 1 < len(hops):
            osend[turn + 1] = tile
            ocopies.append(
                remote(
                    osend.at[turn + 1],
                    orecv.at[turn + 1],
                    os_sem.at[turn + 1],
                    or_sem.at[turn + 1],
                    hops[turn + 1],
                )
            )
            ocopies[turn + 1].start()
        else:
            om_out[...] = tile

    def gram(hs):
        sr = jnp.zeros((width, width), F32)
        si = jnp.zeros((width, width), F32)
        for h in hs:
            ar, ai = xb[h, 0], xb[h, 1]
            sr = sr + mmt(ar, ar) + mmt(ai, ai)
            si = si + mmt(ar, ai) - mmt(ai, ar)
        return sr, si

    for e in range(PARTS):
        for i in range(ncol - 1):
            xcopies[i * PARTS + e].wait_recv()
        hs = range(e * group, (e + 1) * group)
        for h in hs:
            for p in range(2):
                v = ufull[h, p].astype(F32) + xsend[h, p].astype(F32)
                for i in range(ncol - 1):
                    v = v + xrecv[i, h, p].astype(F32)
                yt[p, :, pl.ds(h * rows, rows)] = v
                xb[h, p] = v.astype(BF)
        sr, si = gram(hs)
        if e == 0:
            hh[0], hh[1] = sr, si
        else:
            hh[0] += sr
            hh[1] += si

    scale = None
    for turn in range(NS_STEPS):
        sr, si = (hh[0], hh[1]) if turn == 0 else gram(range(ncol))
        if turn == 0:
            trace = jnp.sum(jnp.where(diag, sr, 0.0), keepdims=True)
            squared = width / (2.0 * trace)
            scale = jnp.sqrt(squared)
            sr, si = sr * squared, si * squared
        er = ((jnp.where(diag, 1.0, 0.0) - sr) / 2.0).astype(BF)
        ei = (-si / 2.0).astype(BF)
        for h in range(ncol):
            span = pl.ds(h * rows, rows)
            ar, ai = xb[h, 0], xb[h, 1]
            vr = yt[0, :, span] + mm(er, ar) + mm(ei, ai)
            vi = yt[1, :, span] + mm(er, ai) - mm(ei, ar)
            if turn == 0:
                vr, vi = vr * scale, vi * scale
            if turn + 1 < NS_STEPS:
                xb[h, 0] = vr.astype(BF)
                xb[h, 1] = vi.astype(BF)
                yt[0, :, span] = vr
                yt[1, :, span] = vi
            else:
                @pl.when(c == h)
                def _():
                    x_out[0] = vr
                    x_out[1] = vi

    fr, fi = rr[0, mine, :], rr[1, mine, :]
    for i in range(ncol - 1):
        gcopies[i].wait_recv()
        fr = fr + grecv[i, 0].astype(F32)
        fi = fi + grecv[i, 1].astype(F32)
    g_out[0] = fr
    g_out[1] = fi

    for copy in list(ncopies.values()) + ucopies + ocopies + gcopies:
        copy.wait_send()
    for copy in list(acopies.values()) + list(xcopies.values()):
        copy.wait_send()


def place(x_ref, g_ref, om_ref, x_out, g_out, om_out):
    x_out[:, 0, :] = x_ref[0].T
    x_out[:, 1, :] = x_ref[1].T
    g_out[...] = g_ref[...]
    om_out[0, 0] = jnp.max(om_ref[...])


def per_device(correlations, gauge, neighbours, shifts):
    kpts = lax.axis_size("ka")
    ncol = lax.axis_size("col")
    _, nslot, _, rows, bands = correlations.shape
    width = gauge.shape[3]
    ut = jnp.transpose(gauge[0], (1, 2, 0))
    rounds = 0
    while 2**rounds < kpts * ncol:
        rounds += 1
    nstep = nslot // ncol
    nsend = nstep * (ncol - 1) * CHUNKS
    share = width // ncol
    vm = pltpu.VMEM
    dma = pltpu.SemaphoreType.DMA
    smem = pl.BlockSpec(memory_space=pltpu.SMEM)
    vmem = pl.BlockSpec(memory_space=pltpu.VMEM)
    x, g, om = pl.pallas_call(
        functools.partial(kernel, kpts, ncol),
        out_shape=(
            jax.ShapeDtypeStruct((2, width, rows), F32),
            jax.ShapeDtypeStruct((2, share, width), F32),
            jax.ShapeDtypeStruct((8, 128), F32),
        ),
        in_specs=[smem, smem, pl.BlockSpec(memory_space=pl.ANY), vmem],
        out_specs=(vmem, vmem, vmem),
        scratch_shapes=[
            vm((nslot, 2, rows, bands), BF),
            vm((nslot, 2, width, rows), BF),
            vm((ncol, 2, width, rows), BF),
            vm((nsend, 2, width // CHUNKS, bands), BF),
            vm((nsend, 2, width // CHUNKS, bands), BF),
            vm((nstep * CHUNKS, 2, width // CHUNKS, bands), F32),
            vm((2, width, bands), F32),
            vm((2, width, width), F32),
            vm((2, width, width), F32),
            vm((2, width, width), F32),
            vm((1, width), F32),
            vm((ncol, 2, width, rows), BF),
            vm((ncol - 1, ncol, 2, width, rows), BF),
            vm((ncol - 1, 2, share, width), BF),
            vm((ncol - 1, 2, share, width), BF),
            vm((ncol, 2, width, rows), BF),
            vm((rounds, 8, 128), F32),
            vm((rounds, 8, 128), F32),
            pltpu.SMEM((nslot,), jnp.int32),
            pltpu.SMEM((nslot,), F32),
            dma((nslot,)),
            dma((nslot,)),
            dma((nslot,)),
            dma((ncol - 1,)),
            dma((ncol - 1,)),
            dma((nsend,)),
            dma((nsend,)),
            dma(((ncol - 1) * PARTS,)),
            dma(((ncol - 1) * PARTS,)),
            dma((ncol - 1,)),
            dma((ncol - 1,)),
            dma((rounds,)),
            dma((rounds,)),
        ],
        compiler_params=pltpu.CompilerParams(
            collective_id=0, has_side_effects=True, vmem_limit_bytes=56 * 1024 * 1024
        ),
    )(neighbours, jnp.transpose(shifts, (2, 0, 1)), correlations, ut)
    x, g, om = pl.pallas_call(
        place,
        out_shape=(
            jax.ShapeDtypeStruct((rows, 2, width), F32),
            jax.ShapeDtypeStruct((2, share, width), F32),
            jax.ShapeDtypeStruct((1, 1), F32),
        ),
        in_specs=[vmem, vmem, vmem],
        out_specs=(vmem, vmem, smem),
    )(x, g, om)
    return (x[None], g[None], om[0, 0])


def solution(mesh):
    return jax.shard_map(
        per_device,
        mesh=mesh,
        in_specs=(
            P("ka", None, None, "col", None),
            P("ka", "col", None, None),
            P("ka", None),
            P("ka", None, None),
        ),
        out_specs=(P("ka", "col", None, None), P("ka", None, "col", None), P()),
        check_vma=False,
    )
```

```python
import functools

import jax
import jax.numpy as jnp
from jax import lax
from jax.experimental import pallas as pl
from jax.experimental.pallas import tpu as pltpu
from jax.sharding import PartitionSpec as P

NS_STEPS = 3
MIXING = 0.02
STEP_LENGTH = 0.2
MESH = pl.DeviceIdType.MESH
CHUNKS = 1
PARTS = 2
SLOTS = [
    (1, 0, 0),
    (-1, 0, 0),
    (0, 0, 1),
    (0, 0, -1),
    (0, 1, 0),
    (0, -1, 0),
    (1, 1, 1),
    (-1, -1, -1),
]
F32 = jnp.float32
BF = jnp.bfloat16


def slot_weight(disp, grid):
    f = [d / n for d, n in zip(disp, grid)]
    x = -f[0] + f[1] + f[2]
    y = f[0] - f[1] + f[2]
    z = f[0] + f[1] - f[2]
    return 3.0 / (len(SLOTS) * (x * x + y * y + z * z))


def mm(a, b):
    return lax.dot_general(a, b, (((1,), (0,)), ((), ())), preferred_element_type=F32)


def mmt(a, b):
    return lax.dot_general(a, b, (((1,), (1,)), ((), ())), preferred_element_type=F32)


def kernel(
    kpts, ncol, nbr_ref, shift_ref, m_hbm, ut_ref,
    x_out, g_out, om_out,
    mbuf, nbuf, ufull, asend, arecv, part, yt, hh, rr, rt, om,
    xsend, xrecv, gsend, grecv, xb, osend, orecv, which, wsm,
    m_sem, ns_sem, nr_sem, us_sem, ur_sem, as_sem, ar_sem, xs_sem, xr_sem, gs_sem, gr_sem,
    os_sem, or_sem,
):
    k = lax.axis_index("ka")
    c = lax.axis_index("col")
    nslot = len(SLOTS)
    nstep = nslot // ncol
    grid = (kpts // 16, 4, 4)
    width = ut_ref.shape[1]
    rows = ut_ref.shape[2]
    others = [lax.rem(c + off, ncol) for off in range(1, ncol)]
    g = (k // 16, k // 4 % 4, k % 4)

    def local_slot(disp):
        return all(d % n == 0 for d, n in zip(disp, grid))

    def moved_to(disp):
        t = [(g[a] - disp[a] + grid[a]) % grid[a] for a in range(3)]
        return t[0] * 16 + t[1] * 4 + t[2]

    bits = []
    step = 1
    while step < kpts:
        bits.append(step)
        step *= 2

    def flip(pos, bit):
        return pos + bit - 2 * bit * (pos // bit % 2)

    hops = [(k, flip(c, bit)) for bit in (1, 2, 4, 8, 16) if bit < ncol]
    hops += [(flip(k, bit), c) for bit in bits]

    for b in range(nslot):
        pltpu.make_async_copy(m_hbm.at[0, b], mbuf.at[b], m_sem.at[b]).start()

    barrier = pltpu.get_barrier_semaphore()
    partners = [(moved_to(d), c) for d in SLOTS if not local_slot(d)]
    partners += [(k, o) for o in others] + hops
    for who in partners:
        pl.semaphore_signal(barrier, inc=1, device_id=who, device_id_type=MESH)
    pl.semaphore_wait(barrier, len(partners))

    def remote(src, dst, s, r, who):
        return pltpu.make_async_remote_copy(
            src_ref=src, dst_ref=dst, send_sem=s, recv_sem=r, device_id=who, device_id_type=MESH
        )

    ucopies = []
    for i, o in enumerate(others):
        ucopies.append(remote(ut_ref, ufull.at[c], us_sem.at[i], ur_sem.at[i], (k, o)))
        ucopies[i].start()
    singles = [s for s, d in enumerate(SLOTS) if sum(map(abs, d)) == 1 and not local_slot(d)]

    def two_hops(disp):
        for e in singles:
            for f in singles:
                fits = [(SLOTS[e][a] + SLOTS[f][a] - disp[a]) % grid[a] == 0 for a in range(3)]
                if SLOTS[e][1] and SLOTS[f][2] and all(fits):
                    return e, SLOTS[f]
        return None

    ncopies = {}
    relays = {}
    arrived = set()

    def arrive(s):
        if s in ncopies and s not in arrived:
            ncopies[s].wait_recv()
            arrived.add(s)

    for s, disp in enumerate(SLOTS):
        if local_slot(disp):
            continue
        if sum(map(abs, disp)) > 1 and two_hops(disp):
            relays[s] = two_hops(disp)
            continue
        ncopies[s] = remote(ut_ref, nbuf.at[s], ns_sem.at[s], nr_sem.at[s], (moved_to(disp), c))
        ncopies[s].start()
    ufull[c] = ut_ref[...]
    for s, disp in enumerate(SLOTS):
        if local_slot(disp):
            nbuf[s] = ut_ref[...]

    codes = []
    for b in range(nslot):
        nb = nbr_ref[0, b]
        gn = (nb // 16, nb // 4 % 4, nb % 4)
        m = [gn[a] - g[a] + shift_ref[a, 0, b] * grid[a] for a in range(3)]
        codes.append(m[0] * 9 + m[1] * 3 + m[2])
    for s, disp in enumerate(SLOTS):
        code = disp[0] * 9 + disp[1] * 3 + disp[2]
        found = jnp.int32(0)
        for b in range(nslot):
            found = jnp.where(codes[b] == code, jnp.int32(b), found)
        which[s] = found
        wsm[s] = jnp.float32(slot_weight(disp, grid))

    for b in range(nslot):
        pltpu.make_async_copy(m_hbm.at[0, b], mbuf.at[b], m_sem.at[b]).wait()

    part_w = width // CHUNKS

    def product(s, q):
        b = which[s]
        cr, ci = mbuf[b, 0], mbuf[b, 1]
        lines = pl.ds(q * part_w, part_w)
        nr, ni = nbuf[s, 0, lines, :], nbuf[s, 1, lines, :]
        return mm(nr, cr) - mm(ni, ci), mm(nr, ci) + mm(ni, cr)

    acopies = {}

    def relay():
        for s, (e, f) in relays.items():
            arrive(e)
            ncopies[s] = remote(
                nbuf.at[e], nbuf.at[s], ns_sem.at[s], nr_sem.at[s], (moved_to(f), c)
            )
            ncopies[s].start()

    def produce(j):
        for s in range(ncol * j, ncol * (j + 1)):
            arrive(s)
        for q in range(CHUNKS):
            for i, o in enumerate(others):
                n = (j * (ncol - 1) + i) * CHUNKS + q
                ar, ai = product(ncol * j + o, q)
                asend[n, 0] = ar.astype(BF)
                asend[n, 1] = ai.astype(BF)
                acopies[n] = remote(
                    asend.at[n], arecv.at[n], as_sem.at[n], ar_sem.at[n], (k, o)
                )
                acopies[n].start()
        for q in range(CHUNKS):
            ar, ai = product(ncol * j + c, q)
            part[j * CHUNKS + q, 0] = ar
            part[j * CHUNKS + q, 1] = ai

    row = lax.broadcasted_iota(jnp.int32, (width, width), 0)
    col = lax.broadcasted_iota(jnp.int32, (width, width), 1)
    diag = row == col

    def consume(j):
        w = wsm[ncol * j + c]
        for q in range(CHUNKS):
            lines = pl.ds(q * part_w, part_w)
            fr, fi = part[j * CHUNKS + q, 0], part[j * CHUNKS + q, 1]
            for i in range(ncol - 1):
                n = (j * (ncol - 1) + i) * CHUNKS + q
                acopies[n].wait_recv()
                fr = fr + arecv[n, 0].astype(F32)
                fi = fi + arecv[n, 1].astype(F32)
            fr, fi = fr.astype(BF), fi.astype(BF)
            tr = jnp.zeros((part_w, width), F32)
            ti = jnp.zeros((part_w, width), F32)
            for h in range(ncol):
                ar, ai = fr[:, h * rows : (h + 1) * rows], fi[:, h * rows : (h + 1) * rows]
                ur, ui = ufull[h, 0], ufull[h, 1]
                tr = tr + mmt(ar, ur) + mmt(ai, ui)
                ti = ti + mmt(ai, ur) - mmt(ar, ui)
            trb, tib = tr.astype(BF), ti.astype(BF)
            tr, ti = trb.astype(F32), tib.astype(F32)
            mr, mi = tr.T, ti.T
            mrb, mib = mr.astype(BF), mi.astype(BF)
            hr = w * (mm(mrb, trb) + mm(mib, tib))
            hi = w * (mm(mib, trb) - mm(mrb, tib))
            down = row[:, :part_w] == col[:, :part_w] + q * part_w
            over = row[:part_w, :] + q * part_w == col[:part_w, :]
            drr = w * jnp.sum(jnp.where(down, mr, 0.0), 0, keepdims=True)
            dri = w * jnp.sum(jnp.where(down, mi, 0.0), 0, keepdims=True)
            dcr = w * jnp.sum(jnp.where(over, tr, 0.0), 1, keepdims=True)
            dci = w * jnp.sum(jnp.where(over, ti, 0.0), 1, keepdims=True)
            rr0, rr1 = mr * drr + mi * dri, mi * drr - mr * dri
            rt0, rt1 = tr * dcr + ti * dci, ti * dcr - tr * dci
            square = jnp.where(over, 0.0, tr * tr + ti * ti)
            omj = w * jnp.sum(square, 0, keepdims=True)
            yr = w * (mm(mrb, fr) + mm(mib, fi))
            yi = w * (mm(mrb, fi) - mm(mib, fr))
            if j == 0:
                rr[0, :, lines], rr[1, :, lines], rt[0, lines, :], rt[1, lines, :] = (
                    rr0, rr1, rt0, rt1,
                )
            else:
                rr[0, :, lines] += rr0
                rr[1, :, lines] += rr1
                rt[0, lines, :] += rt0
                rt[1, lines, :] += rt1
            if j == 0 and q == 0:
                hh[0], hh[1], om[...], yt[0], yt[1] = hr, hi, omj, yr, yi
            else:
                hh[0] += hr
                hh[1] += hi
                om[...] += omj
                yt[0] += yr
                yt[1] += yi

    for j in range(nstep):
        produce(j)
        if j == 0:
            for ucopy in ucopies:
                ucopy.wait_recv()
        else:
            if j == 1:
                relay()
            consume(j - 1)
    consume(nstep - 1)

    total = jnp.sum(om[...]) / (kpts * width)
    osend[0] = jnp.full(osend.shape[1:], total, F32)
    ocopies = [remote(osend.at[0], orecv.at[0], os_sem.at[0], or_sem.at[0], hops[0])]
    ocopies[0].start()
    rr[0] = 2.0 * (rr[0] - rt[0])
    rr[1] = 2.0 * (rr[1] + rt[1])
    kr = (-STEP_LENGTH * rr[0] - MIXING * hh[0]).astype(BF)
    ki = (STEP_LENGTH * rr[1] + MIXING * hh[1]).astype(BF)
    xcopies = {}
    group = ncol // PARTS
    for h in range(ncol):
        span = pl.ds(h * rows, rows)
        ur, ui = ufull[h, 0], ufull[h, 1]
        xsend[h, 0] = (MIXING * yt[0, :, span] + mm(kr, ur) - mm(ki, ui)).astype(BF)
        xsend[h, 1] = (MIXING * yt[1, :, span] + mm(kr, ui) + mm(ki, ur)).astype(BF)
        if h % group == group - 1:
            e = h // group
            piece = pl.ds(e * group, group)
            for i, o in enumerate(others):
                n = i * PARTS + e
                xcopies[n] = remote(
                    xsend.at[piece], xrecv.at[i, piece], xs_sem.at[n], xr_sem.at[n], (k, o)
                )
                xcopies[n].start()
    share = width // ncol
    mine = pl.ds(pl.multiple_of(c * share, share), share)
    gcopies = []
    for i, o in enumerate(others):
        theirs = pl.ds(pl.multiple_of(o * share, share), share)
        gsend[i, 0] = rr[0, theirs, :].astype(BF)
        gsend[i, 1] = rr[1, theirs, :].astype(BF)
        gcopies.append(remote(gsend.at[i], grecv.at[i], gs_sem.at[i], gr_sem.at[i], (k, o)))
        gcopies[i].start()

    for turn in range(len(hops)):
        ocopies[turn].wait_recv()
        tile = osend[turn] + orecv[turn]
        if turn + 1 < len(hops):
            osend[turn + 1] = tile
            ocopies.append(
                remote(
                    osend.at[turn + 1],
                    orecv.at[turn + 1],
                    os_sem.at[turn + 1],
                    or_sem.at[turn + 1],
                    hops[turn + 1],
                )
            )
            ocopies[turn + 1].start()
        else:
            om_out[...] = tile

    def gram(hs):
        sr = jnp.zeros((width, width), F32)
        si = jnp.zeros((width, width), F32)
        for h in hs:
            ar, ai = xb[h, 0], xb[h, 1]
            sr = sr + mmt(ar, ar) + mmt(ai, ai)
            si = si + mmt(ar, ai) - mmt(ai, ar)
        return sr, si

    for e in range(PARTS):
        for i in range(ncol - 1):
            xcopies[i * PARTS + e].wait_recv()
        hs = range(e * group, (e + 1) * group)
        for h in hs:
            for p in range(2):
                v = ufull[h, p].astype(F32) + xsend[h, p].astype(F32)
                for i in range(ncol - 1):
                    v = v + xrecv[i, h, p].astype(F32)
                yt[p, :, pl.ds(h * rows, rows)] = v
                xb[h, p] = v.astype(BF)
        sr, si = gram(hs)
        if e == 0:
            hh[0], hh[1] = sr, si
        else:
            hh[0] += sr
            hh[1] += si

    scale = None
    for turn in range(NS_STEPS):
        sr, si = (hh[0], hh[1]) if turn == 0 else gram(range(ncol))
        if turn == 0:
            trace = jnp.sum(jnp.where(diag, sr, 0.0), keepdims=True)
            squared = width / (2.0 * trace)
            scale = jnp.sqrt(squared)
            sr, si = sr * squared, si * squared
        er = ((jnp.where(diag, 1.0, 0.0) - sr) / 2.0).astype(BF)
        ei = (-si / 2.0).astype(BF)
        for h in range(ncol):
            span = pl.ds(h * rows, rows)
            ar, ai = xb[h, 0], xb[h, 1]
            vr = yt[0, :, span] + mm(er, ar) + mm(ei, ai)
            vi = yt[1, :, span] + mm(er, ai) - mm(ei, ar)
            if turn == 0:
                vr, vi = vr * scale, vi * scale
            if turn + 1 < NS_STEPS:
                xb[h, 0] = vr.astype(BF)
                xb[h, 1] = vi.astype(BF)
                yt[0, :, span] = vr
                yt[1, :, span] = vi
            else:
                @pl.when(c == h)
                def _():
                    x_out[0] = vr
                    x_out[1] = vi

    fr, fi = rr[0, mine, :], rr[1, mine, :]
    for i in range(ncol - 1):
        gcopies[i].wait_recv()
        fr = fr + grecv[i, 0].astype(F32)
        fi = fi + grecv[i, 1].astype(F32)
    g_out[0] = fr
    g_out[1] = fi

    for copy in list(ncopies.values()) + ucopies + ocopies + gcopies:
        copy.wait_send()
    for copy in list(acopies.values()) + list(xcopies.values()):
        copy.wait_send()


def place(x_ref, g_ref, om_ref, x_out, g_out, om_out):
    x_out[:, 0, :] = x_ref[0].T
    x_out[:, 1, :] = x_ref[1].T
    g_out[...] = g_ref[...]
    om_out[0, 0] = jnp.max(om_ref[...])


def per_device(correlations, gauge, neighbours, shifts):
    kpts = lax.axis_size("ka")
    ncol = lax.axis_size("col")
    _, nslot, _, rows, bands = correlations.shape
    width = gauge.shape[3]
    ut = jnp.transpose(gauge[0], (1, 2, 0))
    rounds = 0
    while 2**rounds < kpts * ncol:
        rounds += 1
    nstep = nslot // ncol
    nsend = nstep * (ncol - 1) * CHUNKS
    share = width // ncol
    vm = pltpu.VMEM
    dma = pltpu.SemaphoreType.DMA
    smem = pl.BlockSpec(memory_space=pltpu.SMEM)
    vmem = pl.BlockSpec(memory_space=pltpu.VMEM)
    x, g, om = pl.pallas_call(
        functools.partial(kernel, kpts, ncol),
        out_shape=(
            jax.ShapeDtypeStruct((2, width, rows), F32),
            jax.ShapeDtypeStruct((2, share, width), F32),
            jax.ShapeDtypeStruct((8, 128), F32),
        ),
        in_specs=[smem, smem, pl.BlockSpec(memory_space=pl.ANY), vmem],
        out_specs=(vmem, vmem, vmem),
        scratch_shapes=[
            vm((nslot, 2, rows, bands), BF),
            vm((nslot, 2, width, rows), BF),
            vm((ncol, 2, width, rows), BF),
            vm((nsend, 2, width // CHUNKS, bands), BF),
            vm((nsend, 2, width // CHUNKS, bands), BF),
            vm((nstep * CHUNKS, 2, width // CHUNKS, bands), F32),
            vm((2, width, bands), F32),
            vm((2, width, width), F32),
            vm((2, width, width), F32),
            vm((2, width, width), F32),
            vm((1, width), F32),
            vm((ncol, 2, width, rows), BF),
            vm((ncol - 1, ncol, 2, width, rows), BF),
            vm((ncol - 1, 2, share, width), BF),
            vm((ncol - 1, 2, share, width), BF),
            vm((ncol, 2, width, rows), BF),
            vm((rounds, 8, 128), F32),
            vm((rounds, 8, 128), F32),
            pltpu.SMEM((nslot,), jnp.int32),
            pltpu.SMEM((nslot,), F32),
            dma((nslot,)),
            dma((nslot,)),
            dma((nslot,)),
            dma((ncol - 1,)),
            dma((ncol - 1,)),
            dma((nsend,)),
            dma((nsend,)),
            dma(((ncol - 1) * PARTS,)),
            dma(((ncol - 1) * PARTS,)),
            dma((ncol - 1,)),
            dma((ncol - 1,)),
            dma((rounds,)),
            dma((rounds,)),
        ],
        compiler_params=pltpu.CompilerParams(
            collective_id=0, has_side_effects=True, vmem_limit_bytes=56 * 1024 * 1024
        ),
    )(neighbours, jnp.transpose(shifts, (2, 0, 1)), correlations, ut)
    x, g, om = pl.pallas_call(
        place,
        out_shape=(
            jax.ShapeDtypeStruct((rows, 2, width), F32),
            jax.ShapeDtypeStruct((2, share, width), F32),
            jax.ShapeDtypeStruct((1, 1), F32),
        ),
        in_specs=[vmem, vmem, vmem],
        out_specs=(vmem, vmem, smem),
    )(x, g, om)
    return (x[None], g[None], om[0, 0])


def solution(mesh):
    return jax.shard_map(
        per_device,
        mesh=mesh,
        in_specs=(
            P("ka", None, None, "col", None),
            P("ka", "col", None, None),
            P("ka", None),
            P("ka", None, None),
        ),
        out_specs=(P("ka", "col", None, None), P("ka", None, "col", None), P()),
        check_vma=False,
    )
```
